32 devices in a mesh: bx: 4 (over z), by: 8 (over y, x, core).
Axes of the slice: x: 2, y: 2, z: 4, core: 2. Of those that a mesh axis runs over, the one named last changes fastest.
Arguments:
- state: float32 [384, 32, 1024], P(None, 'bx', 'by'), may hold values from -6 to 6
- target: bfloat16 [384, 32, 1024], P(None, 'bx', 'by'), may hold values from -6 to 6
- land_mask: int32 [32, 1024], P('bx', 'by'), may hold values 0 or 1
- batch_map: int32 [32, 1024], P('bx', 'by'), may hold values from 0 to 63
- diffusion: float32 [384], replicated, may hold values from 0.05 to 0.2
- speed_x: float32 [384], replicated, may hold values from -0.3 to 0.3
- speed_y: float32 [384], replicated, may hold values from -0.3 to 0.3
- w_in: bfloat16 [384, 4096], replicated, may hold values from -0.3125 to 0.3125
- w_out: bfloat16 [4096, 384], replicated, may hold values from -0.09375 to 0.09375
Outputs:
- new_state: float32 [384, 32, 1024], P(None, 'bx', 'by')
- grad_in: float32 [4096, 384], P(('bx', 'by'))
- grad_out: float32 [4096, 384], P(('bx', 'by'))
- batch_loss: float32 [64], replicated
The draws below stay inside these ranges and needn't reach their ends.
All inputs are finite; a program needn't handle non-finite values. No bound on the sum of `land_mask` on one device may be relied on, other than what follows from the above.
Results may differ from the reference program's by a relative error of at most 0.0017.
Values sent between devices are 32-bit elements; how exact they have to be, the bound alone decides.
A program may use at most 128 MiB of HBM per device.

```python
import jax
import jax.numpy as jnp
from jax import lax

HID = 4096
SUB = 3
BATCHES = 64
V = 384
NX = 32
NY = 1024


def touch_ends(values, key, smallest, top_value):
    extent = values.shape
    spot = [jax.random.randint(jax.random.fold_in(key, axis), (), 0, extent[axis]) for axis in range(len(extent))]
    values = values.at[tuple(spot)].set(smallest)
    longest = extent.index(max(extent))
    spot[longest] = (spot[longest] + 1) % extent[longest]
    return values.at[tuple(spot)].set(top_value)


def block_levels(stream_key, extent, shards, smallest, top_value):
    def one(axis_at, shards_of):
        heights = jax.random.uniform(jax.random.fold_in(jax.random.fold_in(stream_key, 6), axis_at), (shards_of,), jnp.float32, smallest / len(shards), top_value / len(shards))
        return jnp.repeat(jnp.exp(heights), extent[axis_at] // shards_of).reshape((-1,) + (1,) * (len(extent) - axis_at - 1))

    loudness = one(*shards[0])
    for cut in shards[1:]:
        loudness = loudness * one(*cut)
    return loudness


def noise(rng, extent, scale, limit, cuts=(), held_as=jnp.bfloat16):
    level = block_levels(rng, extent, cuts, -0.22, 0.18) if cuts else 1.0
    entries = jax.random.normal(rng, extent, jnp.float32) * scale * level
    return jnp.minimum(jnp.maximum(entries, -limit), limit).astype(held_as)


def setup_inputs(seed: int = 0) -> dict:
    streams_of = jax.random.split(jax.random.key(seed), 10)
    return {
        "state": noise(streams_of[0], (V, NX, NY), 1.0, 6.0, ((1, 4), (2, 8)), jnp.float32),
        "target": noise(streams_of[1], (V, NX, NY), 1.0, 6.0, ((1, 4), (2, 8))),
        "land_mask": touch_ends((jax.random.randint(streams_of[2], (NX, NY), 0, 2) < 1).astype(jnp.int32), jax.random.fold_in(streams_of[2], 1), 0, 1),
        "batch_map": touch_ends(jax.random.randint(streams_of[3], (NX, NY), 0, BATCHES), jax.random.fold_in(streams_of[3], 1), 0, BATCHES - 1).astype(jnp.int32),
        "diffusion": jnp.clip(jax.random.uniform(streams_of[4], (V,), jnp.float32, 0.05, 0.2), 0.05, 0.2),
        "speed_x": jnp.clip(jax.random.uniform(streams_of[5], (V,), jnp.float32, -0.3, 0.3), -0.3, 0.3),
        "speed_y": jnp.clip(jax.random.uniform(streams_of[6], (V,), jnp.float32, -0.3, 0.3), -0.3, 0.3),
        "w_in": noise(streams_of[7], (V, HID), V ** -0.5, 0.3125),
        "w_out": noise(streams_of[8], (HID, V), HID ** -0.5, 0.09375),
    }


def transport(field, diffusion, speed_x, speed_y):
    kap = diffusion[:, None, None]
    sxx = speed_x[:, None, None]
    syy = speed_y[:, None, None]
    padded = jnp.pad(field, ((0, 0), (1, 1), (1, 1)))
    centre = padded[:, 1:-1, 1:-1]
    east = padded[:, 2:, 1:-1]
    west = padded[:, :-2, 1:-1]
    north = padded[:, 1:-1, 2:]
    south = padded[:, 1:-1, :-2]
    return centre + kap * (east + west + north + south - 4.0 * centre) - 0.5 * sxx * (east - west) - 0.5 * syy * (north - south)


def reference(state, target, land_mask, batch_map, diffusion, speed_x, speed_y, w_in, w_out):
    field = state
    for substep in range(SUB):
        field = transport(field, diffusion, speed_x, speed_y)
    total = NX * NY
    inputs = field.reshape(V, total).T.astype(jnp.bfloat16)
    pre = jnp.dot(inputs, w_in, preferred_element_type=jnp.float32)
    hidden = jax.nn.silu(pre).astype(jnp.bfloat16)
    tend = jnp.dot(hidden, w_out, preferred_element_type=jnp.float32)
    weights = land_mask.reshape(total).astype(jnp.float32)[:, None]
    err = weights * (tend - target.reshape(V, total).T.astype(jnp.float32))
    new_state = field + 0.5 * (weights * tend).T.reshape(V, NX, NY)
    persq = 0.5 * jnp.sum(err * err, axis=1)
    onehot = (batch_map.reshape(total)[:, None] == jnp.arange(BATCHES, dtype=jnp.int32)[None, :]).astype(jnp.float32)
    batch_loss = jnp.dot(persq, onehot, precision=lax.Precision.HIGHEST) * (BATCHES / (total * V))
    dtend = (err * (total ** -0.5)).astype(jnp.bfloat16)
    dhid = jnp.dot(dtend, w_out.T, preferred_element_type=jnp.float32)
    sig = jax.nn.sigmoid(pre)
    dpre = (dhid * sig * (1.0 + pre * (1.0 - sig))).astype(jnp.bfloat16)
    grad_out = jnp.dot(hidden.T, dtend, preferred_element_type=jnp.float32)
    grad_in = jnp.dot(dpre.T, inputs, preferred_element_type=jnp.float32)
    return new_state, grad_in, grad_out, batch_loss
```

```python
import functools

import jax
import jax.numpy as jnp
from jax import lax
from jax.experimental import pallas as pl
from jax.experimental.pallas import tpu as pltpu
from jax.sharding import PartitionSpec as P

SUB = 3
BATCHES = 64
CHUNKS = 4
MESH = pl.DeviceIdType.MESH
F32 = jnp.float32
BF16 = jnp.bfloat16


def extended(cells, sides, width):
    for axis, dim in sides:
        count = lax.axis_size(axis)
        ends = count - 1
        head = lax.slice_in_dim(cells, 0, width, axis=dim)
        tail = lax.slice_in_dim(cells, cells.shape[dim] - width, cells.shape[dim], axis=dim)
        cells = jnp.concatenate(
            [
                lax.ppermute(tail, axis, [(i, (i + 1) % count) for i in range(ends)]),
                cells,
                lax.ppermute(head, axis, [((i + 1) % count, i) for i in range(ends)]),
            ],
            axis=dim,
        )
    return cells


def advance(padded, kap, sxx, syy):
    centre = padded[:, 1:-1, 1:-1]
    east = padded[:, 2:, 1:-1]
    west = padded[:, :-2, 1:-1]
    north = padded[:, 1:-1, 2:]
    south = padded[:, 1:-1, :-2]
    return (
        centre
        + kap * (east + west + north + south - 4.0 * centre)
        - 0.5 * sxx * (east - west)
        - 0.5 * syy * (north - south)
    )


def transported(state, diffusion, speed_x, speed_y):
    feats, rows_x, rows_y = state.shape
    kap = diffusion[:, None, None]
    sxx = speed_x[:, None, None]
    syy = speed_y[:, None, None]
    field = extended(state, (("bx", 1), ("by", 2)), SUB)
    for substep in range(SUB):
        field = advance(field, kap, sxx, syy)
        margin = SUB - substep - 1
        if margin > 0:
            along_x = (
                lax.axis_index("bx") * rows_x
                + jnp.arange(rows_x + 2 * margin, dtype=jnp.int32)
                - margin
            )
            along_y = (
                lax.axis_index("by") * rows_y
                + jnp.arange(rows_y + 2 * margin, dtype=jnp.int32)
                - margin
            )
            inside_x = ((along_x >= 0) & (along_x < rows_x * lax.axis_size("bx"))).astype(F32)
            inside_y = ((along_y >= 0) & (along_y < rows_y * lax.axis_size("by"))).astype(F32)
            field = field * inside_x[None, :, None] * inside_y[None, None, :]
    return field


def tree(parts):
    if len(parts) == 1:
        return parts[0]
    return tree(parts[::2]) + tree(parts[1::2])


def backward_kernel(
    zs, bs, gathered,
    x_ref, xt_ref, d_ref, dt_ref, wi_ref, wo_ref, loss_ref,
    gin_ref, gout_ref, total_ref,
    g0, g1, c0, c1, q0, q1, a0, a1, z0, z1, lc, lq, la, lz,
    send, recv, lsend, lrecv,
):
    quads = bs // 4
    me_z, me_b = lax.axis_index("bx"), lax.axis_index("by")
    core, q, a = lax.rem(me_b, 2), lax.rem(me_b // 2, 2), me_b // 4
    rows, feats = g0.shape[-2:]
    grads, cores, qs, quadss, zz = (g0, g1), (c0, c1), (q0, q1), (a0, a1), (z0, z1)
    outs = (gout_ref, gin_ref)

    def other_a(s):
        return lax.rem(a + s, quads)

    def other_z(s):
        return lax.rem(me_z + s, zs)

    core_peer = (me_z, me_b + 1 - 2 * core)
    q_peer = (me_z, me_b + 2 - 4 * q)
    a_peers = [(me_z, other_a(s) * 4 + lax.rem(me_b, 4)) for s in range(1, quads)]
    z_peers = [(other_z(s), me_b) for s in range(1, zs)]
    everyone = [core_peer, q_peer] + a_peers + z_peers

    barrier = pltpu.get_barrier_semaphore()
    for peer in everyone:
        pl.semaphore_signal(barrier, inc=1, device_id=peer, device_id_type=MESH)

    def remote(src, dst, peer, ssem, rsem):
        return pltpu.make_async_remote_copy(
            src_ref=src, dst_ref=dst, send_sem=ssem, recv_sem=rsem,
            device_id=peer, device_id_type=MESH,
        )

    kq, ka, kz = 1, 2, 2 + quads - 1

    def copies(stage, m, c):
        def one(src, dst, peer, k):
            return remote(src, dst, peer, send.at[c, m, k], recv.at[c, m, k])

        if stage == 0:
            return [one(grads[m].at[c, :, :, :, 1 - core], cores[m].at[c], core_peer, 0)]
        if stage == 3:
            held = a0.at[c, 0] if m == 0 else q1.at[c]
            return [
                one(held.at[other_z(s)], zz[m].at[c, s - 1], z_peers[s - 1], kz + s - 1)
                for s in range(1, zs)
            ]
        if (m == 0) == (stage == 1):
            src = c0.at[c, :, :, 1 - q] if m == 0 else a1.at[c, 0, :, 1 - q]
            return [one(src, qs[m].at[c], q_peer, kq)]
        held = q0 if m == 0 else c1
        return [
            one(held.at[c, :, other_a(s)], quadss[m].at[c, s - 1], a_peers[s - 1], ka + s - 1)
            for s in range(1, quads)
        ]

    def gather_sum(stage, m, c):
        if stage == 0:
            @pl.loop(0, zs)
            def _(z):
                cores[m][c, z] = cores[m][c, z] + grads[m][c, z, :, :, core]
        elif stage == 3:
            own = a0[c, 0, me_z] if m == 0 else q1[c, me_z]
            outs[m][c * rows:(c + 1) * rows] = tree(
                [own] + [zz[m][c, s] for s in range(zs - 1)]
            )
        elif (m == 0) == (stage == 1):
            own = c0[c, :, :, q] if m == 0 else a1[c, 0, :, q]
            qs[m][c] = qs[m][c] + own
        else:
            own = q0[c, :, a] if m == 0 else c1[c, :, a]
            quadss[m][c, 0] = tree([own] + [quadss[m][c, s] for s in range(quads - 1)])

    def loss_copies(stage):
        if stage == 0:
            return [remote(loss_ref, lc, core_peer, lsend.at[0], lrecv.at[0])]
        if stage == 1:
            return [remote(lc, lq, q_peer, lsend.at[1], lrecv.at[1])]
        if stage == 2:
            return [
                remote(lq, la.at[s - 1], a_peers[s - 1], lsend.at[ka + s - 1], lrecv.at[ka + s - 1])
                for s in range(1, quads)
            ]
        return [
            remote(la.at[0], lz.at[s - 1], z_peers[s - 1], lsend.at[kz + s - 1], lrecv.at[kz + s - 1])
            for s in range(1, zs)
        ]

    def loss_sum(stage):
        if stage == 0:
            lc[...] = lc[...] + loss_ref[...]
        elif stage == 1:
            lq[...] = lq[...] + lc[...]
        elif stage == 2:
            la[0] = tree([lq[...]] + [la[s] for s in range(quads - 1)])
        else:
            total_ref[...] = tree([la[0]] + [lz[s] for s in range(zs - 1)])

    def compute(c):
        @pl.loop(0, zs)
        def _(z):
            if gathered:
                wi = wi_ref[pl.ds(z * bs, bs), c].reshape(bs * rows, feats)
                wo = wo_ref[pl.ds(z * bs, bs), c].reshape(bs * rows, feats)
            else:
                wi, wo = wi_ref[c * zs + z], wo_ref[c * zs + z]
            pre = jnp.dot(wi, xt_ref[...], preferred_element_type=F32)
            sig = jax.nn.sigmoid(pre)
            hidden = (pre * sig).astype(BF16)
            g0[c, z] = jnp.dot(hidden, d_ref[...], preferred_element_type=F32).reshape(
                quads, 2, 2, rows, feats
            )
            dhid = jnp.dot(wo, dt_ref[...], preferred_element_type=F32)
            dpre = (dhid * sig * (1.0 + pre * (1.0 - sig))).astype(BF16)
            g1[c, z] = jnp.dot(dpre, x_ref[...], preferred_element_type=F32).reshape(
                quads, 2, 2, rows, feats
            )

    started = []

    def begin(group):
        for copy in group:
            copy.start()
            started.append(copy)
        return group

    flying = {}
    for step in range(CHUNKS + 4):
        if step < CHUNKS:
            compute(step)
            if step == 0:
                pl.semaphore_wait(barrier, len(everyone))
            for m in range(2):
                flying[0, m, step] = begin(copies(0, m, step))
        if step == 0:
            flying["loss", 0] = begin(loss_copies(0))
        for stage in range(4):
            c = step - 1 - stage
            if not 0 <= c < CHUNKS:
                continue
            for m in range(2):
                for copy in flying[stage, m, c]:
                    copy.wait_recv()
                gather_sum(stage, m, c)
                if stage < 3:
                    flying[stage + 1, m, c] = begin(copies(stage + 1, m, c))
            if c == 0:
                for copy in flying["loss", stage]:
                    copy.wait_recv()
                if stage == 2:
                    loss_sum(stage)
                    flying["loss", 3] = begin(loss_copies(3))
                else:
                    loss_sum(stage)
                    if stage < 3:
                        flying["loss", stage + 1] = begin(loss_copies(stage + 1))
    for copy in started:
        copy.wait_send()


def backward(x, xt, d, dt, wi, wo, partial_loss):
    zs, bs = lax.axis_size("bx"), lax.axis_size("by")
    quads = bs // 4
    hid, feats = wo.shape
    blocks = zs * bs
    rows = hid // blocks // CHUNKS
    gathered = rows % 16 == 0
    wi = wi.T.reshape(blocks, CHUNKS, rows, feats)
    wo = wo.reshape(blocks, CHUNKS, rows, feats)
    if not gathered:
        wi, wo = (
            w.transpose(1, 0, 2, 3).reshape(CHUNKS * zs, bs * rows, feats) for w in (wi, wo)
        )
    kinds = 2 + (quads - 1) + (zs - 1)
    vmem = pl.BlockSpec(memory_space=pltpu.VMEM)
    tile = partial_loss.shape

    def buf(*shape):
        return pltpu.VMEM((CHUNKS,) + shape + (rows, feats), F32)

    grad = jax.ShapeDtypeStruct((rows * CHUNKS, feats), F32)
    return pl.pallas_call(
        functools.partial(backward_kernel, zs, bs, gathered),
        out_shape=(grad, grad, jax.ShapeDtypeStruct(tile, F32)),
        in_specs=[vmem] * 7,
        out_specs=(vmem,) * 3,
        scratch_shapes=[
            buf(zs, quads, 2, 2), buf(zs, quads, 2, 2),
            buf(zs, quads, 2), buf(zs, quads, 2),
            buf(zs, quads), buf(zs),
            buf(quads - 1, zs), buf(quads - 1, zs, 2),
            buf(zs - 1), buf(zs - 1),
            pltpu.VMEM(tile, F32), pltpu.VMEM(tile, F32),
            pltpu.VMEM((quads - 1,) + tile, F32), pltpu.VMEM((zs - 1,) + tile, F32),
            pltpu.SemaphoreType.DMA((CHUNKS, 2, kinds)),
            pltpu.SemaphoreType.DMA((CHUNKS, 2, kinds)),
            pltpu.SemaphoreType.DMA((kinds,)),
            pltpu.SemaphoreType.DMA((kinds,)),
        ],
        compiler_params=pltpu.CompilerParams(collective_id=0, has_side_effects=True),
    )(x, xt, d, dt, wi, wo, partial_loss)


def on_device(state, target, land_mask, batch_map, diffusion, speed_x, speed_y, w_in, w_out):
    feats, rows_x, rows_y = state.shape
    field = transported(state, diffusion, speed_x, speed_y)
    local_cols = rows_x * rows_y
    total = local_cols * lax.axis_size("bx") * lax.axis_size("by")
    flat = field.reshape(feats, local_cols)
    xt = flat.astype(BF16)
    x = xt.T
    pre = jnp.dot(x, w_in, preferred_element_type=F32)
    hidden = jax.nn.silu(pre).astype(BF16)
    tend = jnp.dot(hidden, w_out, preferred_element_type=F32).T
    weights = land_mask.reshape(local_cols).astype(F32)[None, :]
    err = weights * (tend - target.reshape(feats, local_cols).astype(F32))
    new_state = (flat + 0.5 * (weights * tend)).reshape(feats, rows_x, rows_y)
    persq = 0.5 * jnp.sum(err * err, axis=0)
    width = -(-BATCHES // 128) * 128
    onehot = (
        batch_map.reshape(local_cols)[:, None] == jnp.arange(width, dtype=jnp.int32)[None, :]
    ).astype(F32)
    partial_loss = jnp.dot(persq, onehot, precision=lax.Precision.HIGHEST) * (
        BATCHES / (total * feats)
    )
    dt = (err * total ** (-0.5)).astype(BF16)
    grad_in, grad_out, loss = backward(
        x, xt, dt.T, dt, w_in, w_out, jnp.broadcast_to(partial_loss[None, :], (8, width))
    )
    return (new_state, grad_in, grad_out, loss[0, :BATCHES])


def solution(mesh):
    placed = (
        P(None, "bx", "by"),
        P(None, "bx", "by"),
        P("bx", "by"),
        P("bx", "by"),
        P(),
        P(),
        P(),
        P(),
        P(),
    )
    return jax.shard_map(
        on_device,
        mesh=mesh,
        in_specs=placed,
        out_specs=(P(None, "bx", "by"), P(("bx", "by"), None), P(("bx", "by"), None), P()),
        check_vma=False,
    )
```

```python
import functools

import jax
import jax.numpy as jnp
from jax import lax
from jax.experimental import pallas as pl
from jax.experimental.pallas import tpu as pltpu
from jax.sharding import PartitionSpec as P

SUB = 3
BATCHES = 64
CHUNKS = 4
MESH = pl.DeviceIdType.MESH
F32 = jnp.float32
BF16 = jnp.bfloat16


WIDE = 8
EDGE = 2 * WIDE
SIDES = [(dx, dy) for dx in (-1, 0, 1) for dy in (-1, 0, 1) if dx or dy]


def halo_kernel(zs, bs, cells, coef, out, first, second, send, recv):
    rows, depth, feats = cells.shape
    me_z, me_b = lax.axis_index("bx"), lax.axis_index("by")
    window = pl.ds(EDGE, depth)

    def has(side):
        dx, dy = side
        found = []
        if dx:
            found.append(me_z > 0 if dx < 0 else me_z < zs - 1)
        if dy:
            found.append(me_b > 0 if dy < 0 else me_b < bs - 1)
        return functools.reduce(jnp.logical_and, found)

    for buf in (first, second):
        for i in range(rows + 2 * SUB):
            buf[i, :EDGE] = jnp.zeros((EDGE, feats), F32)
            buf[i, EDGE + depth:] = jnp.zeros((EDGE, feats), F32)
    for i in list(range(SUB)) + list(range(rows + SUB, rows + 2 * SUB)):
        first[i, window] = jnp.zeros((depth, feats), F32)

    barrier = pltpu.get_barrier_semaphore()
    for dx, dy in SIDES:
        @pl.when(has((dx, dy)))
        def _():
            pl.semaphore_signal(
                barrier, inc=1, device_id=(me_z + dx, me_b + dy), device_id_type=MESH
            )
    near_z = jnp.where(me_z > 0, 1, 0) + jnp.where(me_z < zs - 1, 1, 0)
    near_b = jnp.where(me_b > 0, 1, 0) + jnp.where(me_b < bs - 1, 1, 0)
    pl.semaphore_wait(barrier, near_z + near_b + near_z * near_b)

    def own(side):
        dx, dy = side
        i = {-1: pl.ds(0, SUB), 0: pl.ds(0, rows), 1: pl.ds(rows - SUB, SUB)}[dx]
        j = {-1: pl.ds(0, WIDE), 0: pl.ds(0, depth), 1: pl.ds(depth - WIDE, WIDE)}[dy]
        return cells.at[i, j]

    def slot(side):
        dx, dy = side
        i = {-1: pl.ds(0, SUB), 0: pl.ds(SUB, rows), 1: pl.ds(SUB + rows, SUB)}[dx]
        j = {-1: pl.ds(WIDE, WIDE), 0: window, 1: pl.ds(EDGE + depth, WIDE)}[dy]
        return first.at[i, j]

    def copy_to(side):
        dx, dy = side
        back = (-dx, -dy)
        return pltpu.make_async_remote_copy(
            src_ref=own(side), dst_ref=slot(back),
            send_sem=send.at[SIDES.index(side)], recv_sem=recv.at[SIDES.index(back)],
            device_id=(me_z + dx, me_b + dy), device_id_type=MESH,
        )

    for side in sorted(SIDES, key=lambda s: (s[1] != 0, s[0] == 0)):
        @pl.when(has(side))
        def _():
            copy_to(side).start()
    for i in range(rows):
        first[SUB + i, window] = cells[i]
    for side in SIDES:
        @pl.when(has(side))
        def _():
            copy_to((-side[0], -side[1])).wait_recv()
    for side in SIDES:
        @pl.when(has(side))
        def _():
            copy_to(side).wait_send()

    kap, sxx, syy = coef[0:1], coef[1:2], coef[2:3]
    low = jnp.where(me_b > 0, 1.0, 0.0).astype(F32)
    high = jnp.where(me_b < bs - 1, 1.0, 0.0).astype(F32)

    def moved(src, i, start, count):
        centre = src[i, pl.ds(start, count)]
        east = src[i + 1, pl.ds(start, count)]
        west = src[i - 1, pl.ds(start, count)]
        north = src[i, pl.ds(start + 1, count)]
        south = src[i, pl.ds(start - 1, count)]
        return (
            centre
            + kap * (east + west + north + south - 4.0 * centre)
            - 0.5 * sxx * (east - west)
            - 0.5 * syy * (north - south)
        )

    for step in range(SUB):
        src, dst = ((first, second), (second, first))[step % 2]
        margin = SUB - step - 1

        @pl.loop(SUB - margin, SUB + rows + margin)
        def _(i):
            if margin == 0:
                out[i - SUB] = moved(src, i, EDGE, depth)
            else:
                at = me_z * rows + i - SUB
                inside = jnp.where((at >= 0) & (at < rows * zs), 1.0, 0.0).astype(F32)
                dst[i, pl.ds(WIDE, WIDE)] = moved(src, i, WIDE, WIDE) * (inside * low)
                dst[i, window] = moved(src, i, EDGE, depth) * inside
                dst[i, pl.ds(EDGE + depth, WIDE)] = moved(src, i, EDGE + depth, WIDE) * (
                    inside * high
                )


def transported(state, diffusion, speed_x, speed_y):
    zs, bs = lax.axis_size("bx"), lax.axis_size("by")
    cells = state.transpose(1, 2, 0)
    rows, depth, feats = cells.shape
    coef = jnp.concatenate(
        [jnp.stack([diffusion, speed_x, speed_y]), jnp.zeros((5, feats), F32)], axis=0
    )
    vmem = pl.BlockSpec(memory_space=pltpu.VMEM)
    padded = pltpu.VMEM((rows + 2 * SUB, depth + 2 * EDGE, feats), F32)
    return pl.pallas_call(
        functools.partial(halo_kernel, zs, bs),
        out_shape=jax.ShapeDtypeStruct(cells.shape, F32),
        in_specs=[vmem] * 2,
        out_specs=vmem,
        scratch_shapes=[
            padded, padded,
            pltpu.SemaphoreType.DMA((len(SIDES),)), pltpu.SemaphoreType.DMA((len(SIDES),)),
        ],
        compiler_params=pltpu.CompilerParams(collective_id=1, has_side_effects=True),
    )(cells, coef)


def tree(parts):
    if len(parts) == 1:
        return parts[0]
    return tree(parts[::2]) + tree(parts[1::2])


def backward_kernel(
    zs, bs, gathered,
    x_ref, xt_ref, d_ref, dt_ref, wi_ref, wo_ref, loss_ref,
    gin_ref, gout_ref, total_ref,
    g0, g1, c0, c1, q0, q1, a0, a1, z0, z1, lc, lq, la, lz,
    send, recv, lsend, lrecv,
):
    quads = bs // 4
    me_z, me_b = lax.axis_index("bx"), lax.axis_index("by")
    core, q, a = lax.rem(me_b, 2), lax.rem(me_b // 2, 2), me_b // 4
    rows, feats = g0.shape[-2:]
    grads, cores, qs, quadss, zz = (g0, g1), (c0, c1), (q0, q1), (a0, a1), (z0, z1)
    outs = (gout_ref, gin_ref)

    def other_a(s):
        return lax.rem(a + s, quads)

    def other_z(s):
        return lax.rem(me_z + s, zs)

    core_peer = (me_z, me_b + 1 - 2 * core)
    q_peer = (me_z, me_b + 2 - 4 * q)
    a_peers = [(me_z, other_a(s) * 4 + lax.rem(me_b, 4)) for s in range(1, quads)]
    z_peers = [(other_z(s), me_b) for s in range(1, zs)]
    everyone = [core_peer, q_peer] + a_peers + z_peers

    barrier = pltpu.get_barrier_semaphore()
    for peer in everyone:
        pl.semaphore_signal(barrier, inc=1, device_id=peer, device_id_type=MESH)

    def remote(src, dst, peer, ssem, rsem):
        return pltpu.make_async_remote_copy(
            src_ref=src, dst_ref=dst, send_sem=ssem, recv_sem=rsem,
            device_id=peer, device_id_type=MESH,
        )

    kq, ka, kz = 1, 2, 2 + quads - 1

    def copies(stage, m, c):
        def one(src, dst, peer, k):
            return remote(src, dst, peer, send.at[c, m, k], recv.at[c, m, k])

        if stage == 0:
            return [one(grads[m].at[c, :, :, :, 1 - core], cores[m].at[c], core_peer, 0)]
        if stage == 3:
            held = a0.at[c, 0] if m == 0 else q1.at[c]
            return [
                one(held.at[other_z(s)], zz[m].at[c, s - 1], z_peers[s - 1], kz + s - 1)
                for s in range(1, zs)
            ]
        if (m == 0) == (stage == 1):
            src = c0.at[c, :, :, 1 - q] if m == 0 else a1.at[c, 0, :, 1 - q]
            return [one(src, qs[m].at[c], q_peer, kq)]
        held = q0 if m == 0 else c1
        return [
            one(held.at[c, :, other_a(s)], quadss[m].at[c, s - 1], a_peers[s - 1], ka + s - 1)
            for s in range(1, quads)
        ]

    def gather_sum(stage, m, c):
        if stage == 0:
            @pl.loop(0, zs)
            def _(z):
                cores[m][c, z] = cores[m][c, z] + grads[m][c, z, :, :, core]
        elif stage == 3:
            own = a0[c, 0, me_z] if m == 0 else q1[c, me_z]
            outs[m][c * rows:(c + 1) * rows] = tree(
                [own] + [zz[m][c, s] for s in range(zs - 1)]
            )
        elif (m == 0) == (stage == 1):
            own = c0[c, :, :, q] if m == 0 else a1[c, 0, :, q]
            qs[m][c] = qs[m][c] + own
        else:
            own = q0[c, :, a] if m == 0 else c1[c, :, a]
            quadss[m][c, 0] = tree([own] + [quadss[m][c, s] for s in range(quads - 1)])

    def loss_copies(stage):
        if stage == 0:
            return [remote(loss_ref, lc, core_peer, lsend.at[0], lrecv.at[0])]
        if stage == 1:
            return [remote(lc, lq, q_peer, lsend.at[1], lrecv.at[1])]
        if stage == 2:
            return [
                remote(lq, la.at[s - 1], a_peers[s - 1], lsend.at[ka + s - 1], lrecv.at[ka + s - 1])
                for s in range(1, quads)
            ]
        return [
            remote(la.at[0], lz.at[s - 1], z_peers[s - 1], lsend.at[kz + s - 1], lrecv.at[kz + s - 1])
            for s in range(1, zs)
        ]

    def loss_sum(stage):
        if stage == 0:
            lc[...] = lc[...] + loss_ref[...]
        elif stage == 1:
            lq[...] = lq[...] + lc[...]
        elif stage == 2:
            la[0] = tree([lq[...]] + [la[s] for s in range(quads - 1)])
        else:
            total_ref[...] = tree([la[0]] + [lz[s] for s in range(zs - 1)])

    def compute(c):
        @pl.loop(0, zs)
        def _(z):
            if gathered:
                wi = wi_ref[pl.ds(z * bs, bs), c].reshape(bs * rows, feats)
                wo = wo_ref[pl.ds(z * bs, bs), c].reshape(bs * rows, feats)
            else:
                wi, wo = wi_ref[c * zs + z], wo_ref[c * zs + z]
            pre = jnp.dot(wi, xt_ref[...], preferred_element_type=F32)
            sig = jax.nn.sigmoid(pre)
            hidden = (pre * sig).astype(BF16)
            g0[c, z] = jnp.dot(hidden, d_ref[...], preferred_element_type=F32).reshape(
                quads, 2, 2, rows, feats
            )
            dhid = jnp.dot(wo, dt_ref[...], preferred_element_type=F32)
            dpre = (dhid * sig * (1.0 + pre * (1.0 - sig))).astype(BF16)
            g1[c, z] = jnp.dot(dpre, x_ref[...], preferred_element_type=F32).reshape(
                quads, 2, 2, rows, feats
            )

    started = []

    def begin(group):
        for copy in group:
            copy.start()
            started.append(copy)
        return group

    flying = {}
    for step in range(CHUNKS + 4):
        if step < CHUNKS:
            compute(step)
            if step == 0:
                pl.semaphore_wait(barrier, len(everyone))
            for m in range(2):
                flying[0, m, step] = begin(copies(0, m, step))
        if step == 0:
            flying["loss", 0] = begin(loss_copies(0))
        for stage in range(4):
            c = step - 1 - stage
            if not 0 <= c < CHUNKS:
                continue
            for m in range(2):
                for copy in flying[stage, m, c]:
                    copy.wait_recv()
                gather_sum(stage, m, c)
                if stage < 3:
                    flying[stage + 1, m, c] = begin(copies(stage + 1, m, c))
            if c == 0:
                for copy in flying["loss", stage]:
                    copy.wait_recv()
                if stage == 2:
                    loss_sum(stage)
                    flying["loss", 3] = begin(loss_copies(3))
                else:
                    loss_sum(stage)
                    if stage < 3:
                        flying["loss", stage + 1] = begin(loss_copies(stage + 1))
    for copy in started:
        copy.wait_send()


def backward(x, xt, d, dt, wi, wo, partial_loss):
    zs, bs = lax.axis_size("bx"), lax.axis_size("by")
    quads = bs // 4
    hid, feats = wo.shape
    blocks = zs * bs
    rows = hid // blocks // CHUNKS
    gathered = rows % 16 == 0
    wi = wi.T.reshape(blocks, CHUNKS, rows, feats)
    wo = wo.reshape(blocks, CHUNKS, rows, feats)
    if not gathered:
        wi, wo = (
            w.transpose(1, 0, 2, 3).reshape(CHUNKS * zs, bs * rows, feats) for w in (wi, wo)
        )
    kinds = 2 + (quads - 1) + (zs - 1)
    vmem = pl.BlockSpec(memory_space=pltpu.VMEM)
    tile = partial_loss.shape

    def buf(*shape):
        return pltpu.VMEM((CHUNKS,) + shape + (rows, feats), F32)

    grad = jax.ShapeDtypeStruct((rows * CHUNKS, feats), F32)
    return pl.pallas_call(
        functools.partial(backward_kernel, zs, bs, gathered),
        out_shape=(grad, grad, jax.ShapeDtypeStruct(tile, F32)),
        in_specs=[vmem] * 7,
        out_specs=(vmem,) * 3,
        scratch_shapes=[
            buf(zs, quads, 2, 2), buf(zs, quads, 2, 2),
            buf(zs, quads, 2), buf(zs, quads, 2),
            buf(zs, quads), buf(zs),
            buf(quads - 1, zs), buf(quads - 1, zs, 2),
            buf(zs - 1), buf(zs - 1),
            pltpu.VMEM(tile, F32), pltpu.VMEM(tile, F32),
            pltpu.VMEM((quads - 1,) + tile, F32), pltpu.VMEM((zs - 1,) + tile, F32),
            pltpu.SemaphoreType.DMA((CHUNKS, 2, kinds)),
            pltpu.SemaphoreType.DMA((CHUNKS, 2, kinds)),
            pltpu.SemaphoreType.DMA((kinds,)),
            pltpu.SemaphoreType.DMA((kinds,)),
        ],
        compiler_params=pltpu.CompilerParams(collective_id=0, has_side_effects=True),
    )(x, xt, d, dt, wi, wo, partial_loss)


def on_device(state, target, land_mask, batch_map, diffusion, speed_x, speed_y, w_in, w_out):
    feats, rows_x, rows_y = state.shape
    field = transported(state, diffusion, speed_x, speed_y)
    local_cols = rows_x * rows_y
    total = local_cols * lax.axis_size("bx") * lax.axis_size("by")
    flat = field.reshape(local_cols, feats)
    x = flat.astype(BF16)
    xt = x.T
    pre = jnp.dot(x, w_in, preferred_element_type=F32)
    hidden = jax.nn.silu(pre).astype(BF16)
    tend = jnp.dot(hidden, w_out, preferred_element_type=F32)
    weights = land_mask.reshape(local_cols).astype(F32)[:, None]
    err = weights * (tend - target.reshape(feats, local_cols).T.astype(F32))
    new_state = (flat + 0.5 * (weights * tend)).T.reshape(feats, rows_x, rows_y)
    persq = 0.5 * jnp.sum(err * err, axis=1)
    width = -(-BATCHES // 128) * 128
    onehot = (
        batch_map.reshape(local_cols)[:, None] == jnp.arange(width, dtype=jnp.int32)[None, :]
    ).astype(F32)
    partial_loss = jnp.dot(persq, onehot, precision=lax.Precision.HIGHEST) * (
        BATCHES / (total * feats)
    )
    d = (err * total ** (-0.5)).astype(BF16)
    grad_in, grad_out, loss = backward(
        x, xt, d, d.T, w_in, w_out, jnp.broadcast_to(partial_loss[None, :], (8, width))
    )
    return (new_state, grad_in, grad_out, loss[0, :BATCHES])


def solution(mesh):
    placed = (
        P(None, "bx", "by"),
        P(None, "bx", "by"),
        P("bx", "by"),
        P("bx", "by"),
        P(),
        P(),
        P(),
        P(),
        P(),
    )
    return jax.shard_map(
        on_device,
        mesh=mesh,
        in_specs=placed,
        out_specs=(P(None, "bx", "by"), P(("bx", "by"), None), P(("bx", "by"), None), P()),
        check_vma=False,
    )
```

```python
import functools

import jax
import jax.numpy as jnp
from jax import lax
from jax.experimental import pallas as pl
from jax.experimental.pallas import tpu as pltpu
from jax.sharding import PartitionSpec as P

SUB = 3
BATCHES = 64
ACROSS_FIRST = ()
MESH = pl.DeviceIdType.MESH
F32 = jnp.float32
BF16 = jnp.bfloat16


WIDE = 8
EDGE = 2 * WIDE
SIDES = [(dx, dy) for dx in (-1, 0, 1) for dy in (-1, 0, 1) if dx or dy]


def halo_kernel(zs, bs, cells, coef, out, first, second, send, recv):
    rows, depth, feats = cells.shape
    me_z, me_b = lax.axis_index("bx"), lax.axis_index("by")
    window = pl.ds(EDGE, depth)

    def has(side):
        dx, dy = side
        found = []
        if dx:
            found.append(me_z > 0 if dx < 0 else me_z < zs - 1)
        if dy:
            found.append(me_b > 0 if dy < 0 else me_b < bs - 1)
        return functools.reduce(jnp.logical_and, found)

    for buf in (first, second):
        for i in range(rows + 2 * SUB):
            buf[i, :EDGE] = jnp.zeros((EDGE, feats), F32)
            buf[i, EDGE + depth:] = jnp.zeros((EDGE, feats), F32)
    for i in list(range(SUB)) + list(range(rows + SUB, rows + 2 * SUB)):
        first[i, window] = jnp.zeros((depth, feats), F32)

    barrier = pltpu.get_barrier_semaphore()
    for dx, dy in SIDES:
        @pl.when(has((dx, dy)))
        def _():
            pl.semaphore_signal(
                barrier, inc=1, device_id=(me_z + dx, me_b + dy), device_id_type=MESH
            )
    near_z = jnp.where(me_z > 0, 1, 0) + jnp.where(me_z < zs - 1, 1, 0)
    near_b = jnp.where(me_b > 0, 1, 0) + jnp.where(me_b < bs - 1, 1, 0)
    pl.semaphore_wait(barrier, near_z + near_b + near_z * near_b)

    def own(side):
        dx, dy = side
        i = {-1: pl.ds(0, SUB), 0: pl.ds(0, rows), 1: pl.ds(rows - SUB, SUB)}[dx]
        j = {-1: pl.ds(0, WIDE), 0: pl.ds(0, depth), 1: pl.ds(depth - WIDE, WIDE)}[dy]
        return cells.at[i, j]

    def slot(side):
        dx, dy = side
        i = {-1: pl.ds(0, SUB), 0: pl.ds(SUB, rows), 1: pl.ds(SUB + rows, SUB)}[dx]
        j = {-1: pl.ds(WIDE, WIDE), 0: window, 1: pl.ds(EDGE + depth, WIDE)}[dy]
        return first.at[i, j]

    def copy_to(side):
        dx, dy = side
        back = (-dx, -dy)
        return pltpu.make_async_remote_copy(
            src_ref=own(side), dst_ref=slot(back),
            send_sem=send.at[SIDES.index(side)], recv_sem=recv.at[SIDES.index(back)],
            device_id=(me_z + dx, me_b + dy), device_id_type=MESH,
        )

    for side in sorted(SIDES, key=lambda s: (s[1] != 0, s[0] == 0)):
        @pl.when(has(side))
        def _():
            copy_to(side).start()
    for i in range(rows):
        first[SUB + i, window] = cells[i]
    for side in SIDES:
        @pl.when(has(side))
        def _():
            copy_to((-side[0], -side[1])).wait_recv()
    for side in SIDES:
        @pl.when(has(side))
        def _():
            copy_to(side).wait_send()

    kap, sxx, syy = coef[0:1], coef[1:2], coef[2:3]
    low = jnp.where(me_b > 0, 1.0, 0.0).astype(F32)
    high = jnp.where(me_b < bs - 1, 1.0, 0.0).astype(F32)

    def moved(src, i, start, count):
        centre = src[i, pl.ds(start, count)]
        east = src[i + 1, pl.ds(start, count)]
        west = src[i - 1, pl.ds(start, count)]
        north = src[i, pl.ds(start + 1, count)]
        south = src[i, pl.ds(start - 1, count)]
        return (
            centre
            + kap * (east + west + north + south - 4.0 * centre)
            - 0.5 * sxx * (east - west)
            - 0.5 * syy * (north - south)
        )

    for step in range(SUB):
        src, dst = ((first, second), (second, first))[step % 2]
        margin = SUB - step - 1

        @pl.loop(SUB - margin, SUB + rows + margin)
        def _(i):
            if margin == 0:
                out[i - SUB] = moved(src, i, EDGE, depth)
            else:
                at = me_z * rows + i - SUB
                inside = jnp.where((at >= 0) & (at < rows * zs), 1.0, 0.0).astype(F32)
                dst[i, pl.ds(WIDE, WIDE)] = moved(src, i, WIDE, WIDE) * (inside * low)
                dst[i, window] = moved(src, i, EDGE, depth) * inside
                dst[i, pl.ds(EDGE + depth, WIDE)] = moved(src, i, EDGE + depth, WIDE) * (
                    inside * high
                )


def transported(state, diffusion, speed_x, speed_y):
    zs, bs = lax.axis_size("bx"), lax.axis_size("by")
    cells = state.transpose(1, 2, 0)
    rows, depth, feats = cells.shape
    coef = jnp.concatenate(
        [jnp.stack([diffusion, speed_x, speed_y]), jnp.zeros((5, feats), F32)], axis=0
    )
    vmem = pl.BlockSpec(memory_space=pltpu.VMEM)
    padded = pltpu.VMEM((rows + 2 * SUB, depth + 2 * EDGE, feats), F32)
    return pl.pallas_call(
        functools.partial(halo_kernel, zs, bs),
        out_shape=jax.ShapeDtypeStruct(cells.shape, F32),
        in_specs=[vmem] * 2,
        out_specs=vmem,
        scratch_shapes=[
            padded, padded,
            pltpu.SemaphoreType.DMA((len(SIDES),)), pltpu.SemaphoreType.DMA((len(SIDES),)),
        ],
        compiler_params=pltpu.CompilerParams(collective_id=1, has_side_effects=True),
    )(cells, coef)


def tree(parts):
    if len(parts) == 1:
        return parts[0]
    return tree(parts[::2]) + tree(parts[1::2])


def chunk_count(block):
    return 8 if block % 64 == 0 else 4


def orders(chunks):
    plan = {}
    for c in range(chunks):
        for m in range(2):
            plane = "qa" if m == 0 else "aq"
            plan[m, c] = "z" + plane if c in ACROSS_FIRST else plane + "z"
    return plan


def layout(zs, bs, chunks):
    size = {"z": zs, "a": bs // 4, "q": 2}
    groups = {}
    for key, order in sorted(orders(chunks).items()):
        groups.setdefault(order, []).append(key)
    shapes = []
    for order, members in sorted(groups.items()):
        left = "zaq"
        for axis in order:
            left = left.replace(axis, "")
            shapes.append((order, (len(members), size[axis] - 1) + tuple(size[k] for k in left)))
    return groups, shapes


def backward_kernel(
    zs, bs, chunks, gathered,
    x_ref, d_ref, wi_ref, wo_ref, loss_ref,
    gin_ref, gout_ref, total_ref,
    g0, g1, c0, c1, lc, lq, la, lz,
    send, recv, lsend, lrecv, *stages,
):
    quads = bs // 4
    size = {"z": zs, "a": quads, "q": 2}
    me_z, me_b = lax.axis_index("bx"), lax.axis_index("by")
    core, q, a = lax.rem(me_b, 2), lax.rem(me_b // 2, 2), me_b // 4
    mine = {"z": me_z, "a": a, "q": q}
    rows, feats = g0.shape[-2:]
    grads, cores = (g0, g1), (c0, c1)
    outs = (gout_ref, gin_ref)
    plan = orders(chunks)
    groups, shapes = layout(zs, bs, chunks)
    landing = {}
    for (order, _), ref in zip(shapes, stages):
        landing.setdefault(order, []).append(ref)

    def other(axis, s):
        return lax.rem(mine[axis] + s, size[axis])

    core_peer = (me_z, me_b + 1 - 2 * core)
    peers = {
        "q": [(me_z, me_b + 2 - 4 * q)],
        "a": [(me_z, other("a", s) * 4 + lax.rem(me_b, 4)) for s in range(1, quads)],
        "z": [(other("z", s), me_b) for s in range(1, zs)],
    }
    everyone = [core_peer] + peers["q"] + peers["a"] + peers["z"]
    base = {"q": 1, "a": 2, "z": 2 + quads - 1}

    barrier = pltpu.get_barrier_semaphore()
    for peer in everyone:
        pl.semaphore_signal(barrier, inc=1, device_id=peer, device_id_type=MESH)

    def remote(src, dst, peer, ssem, rsem):
        return pltpu.make_async_remote_copy(
            src_ref=src, dst_ref=dst, send_sem=ssem, recv_sem=rsem,
            device_id=peer, device_id_type=MESH,
        )

    def held(stage, m, c):
        if stage == 1:
            return cores[m], (c,), "zaq"
        order = plan[m, c]
        left = "".join(k for k in "zaq" if k not in order[: stage - 1])
        return landing[order][stage - 2], (groups[order].index((m, c)), 0), left

    def part(lead, left, axis, at):
        return lead + tuple(at if k == axis else slice(None) for k in left)

    def copies(stage, m, c):
        if stage == 0:
            return [
                remote(
                    grads[m].at[c, :, :, :, 1 - core], cores[m].at[c], core_peer,
                    send.at[c, m, 0], recv.at[c, m, 0],
                )
            ]
        order = plan[m, c]
        axis = order[stage - 1]
        ref, lead, left = held(stage, m, c)
        spot = groups[order].index((m, c))
        return [
            remote(
                ref.at[part(lead, left, axis, other(axis, s))],
                landing[order][stage - 1].at[spot, s - 1],
                peers[axis][s - 1],
                send.at[c, m, base[axis] + s - 1], recv.at[c, m, base[axis] + s - 1],
            )
            for s in range(1, size[axis])
        ]

    def gather_sum(stage, m, c):
        if stage == 0:
            @pl.loop(0, zs)
            def _(z):
                cores[m][c, z] = cores[m][c, z] + grads[m][c, z, :, :, core]
            return
        order = plan[m, c]
        axis = order[stage - 1]
        ref, lead, left = held(stage, m, c)
        spot = groups[order].index((m, c))
        came = landing[order][stage - 1]
        summed = tree(
            [ref[part(lead, left, axis, mine[axis])]]
            + [came[spot, s] for s in range(size[axis] - 1)]
        )
        if stage == 3:
            outs[m][c * rows:(c + 1) * rows] = summed
        else:
            came[spot, 0] = summed

    loss_axes = "qaz"
    loss_from = [loss_ref, lc, lq.at[0], la.at[0]]
    loss_into = [lc, lq, la, lz]

    def loss_copies(stage):
        if stage == 0:
            return [remote(loss_ref, lc, core_peer, lsend.at[0], lrecv.at[0])]
        axis = loss_axes[stage - 1]
        return [
            remote(
                loss_from[stage], loss_into[stage].at[s - 1], peers[axis][s - 1],
                lsend.at[base[axis] + s - 1], lrecv.at[base[axis] + s - 1],
            )
            for s in range(1, size[axis])
        ]

    def loss_sum(stage):
        if stage == 0:
            lc[...] = lc[...] + loss_ref[...]
            return
        came = loss_into[stage]
        summed = tree(
            [loss_from[stage][...]]
            + [came[s] for s in range(size[loss_axes[stage - 1]] - 1)]
        )
        if stage == 3:
            total_ref[...] = summed
        else:
            came[0] = summed

    def transposed_dot(lhs, rhs):
        return lax.dot_general(lhs, rhs, (((1,), (1,)), ((), ())), preferred_element_type=F32)

    def compute(c):
        @pl.loop(0, zs)
        def _(z):
            if gathered:
                wi = wi_ref[pl.ds(z * bs, bs), c].reshape(bs * rows, feats)
                wo = wo_ref[pl.ds(z * bs, bs), c].reshape(bs * rows, feats)
            else:
                wi, wo = wi_ref[c * zs + z], wo_ref[c * zs + z]
            pre = transposed_dot(wi, x_ref[...])
            sig = jax.nn.sigmoid(pre)
            hidden = (pre * sig).astype(BF16)
            g0[c, z] = jnp.dot(hidden, d_ref[...], preferred_element_type=F32).reshape(
                quads, 2, 2, rows, feats
            )
            dhid = transposed_dot(wo, d_ref[...])
            dpre = (dhid * sig * (1.0 + pre * (1.0 - sig))).astype(BF16)
            g1[c, z] = jnp.dot(dpre, x_ref[...], preferred_element_type=F32).reshape(
                quads, 2, 2, rows, feats
            )

    started = []

    def begin(group):
        for copy in group:
            copy.start()
            started.append(copy)
        return group

    flying = {}
    for step in range(chunks + 4):
        if step < chunks:
            compute(step)
            if step == 0:
                pl.semaphore_wait(barrier, len(everyone))
            for m in range(2):
                flying[0, m, step] = begin(copies(0, m, step))
        if step == 0:
            flying["loss", 0] = begin(loss_copies(0))
        for stage in range(4):
            c = step - 1 - stage
            if not 0 <= c < chunks:
                continue
            for m in range(2):
                for copy in flying[stage, m, c]:
                    copy.wait_recv()
                gather_sum(stage, m, c)
                if stage < 3:
                    flying[stage + 1, m, c] = begin(copies(stage + 1, m, c))
            if c == 0:
                for copy in flying["loss", stage]:
                    copy.wait_recv()
                loss_sum(stage)
                if stage < 3:
                    flying["loss", stage + 1] = begin(loss_copies(stage + 1))
    for copy in started:
        copy.wait_send()


def backward(x, d, wi, wo, partial_loss):
    zs, bs = lax.axis_size("bx"), lax.axis_size("by")
    quads = bs // 4
    hid, feats = wo.shape
    blocks = zs * bs
    chunks = chunk_count(hid // blocks)
    rows = hid // blocks // chunks
    gathered = rows % 16 == 0
    wi = wi.T.reshape(blocks, chunks, rows, feats)
    wo = wo.reshape(blocks, chunks, rows, feats)
    if not gathered:
        wi, wo = (
            w.transpose(1, 0, 2, 3).reshape(chunks * zs, bs * rows, feats) for w in (wi, wo)
        )
    kinds = 2 + (quads - 1) + (zs - 1)
    vmem = pl.BlockSpec(memory_space=pltpu.VMEM)
    tile = partial_loss.shape

    def buf(*shape):
        return pltpu.VMEM(shape + (rows, feats), F32)

    grad = jax.ShapeDtypeStruct((rows * chunks, feats), F32)
    return pl.pallas_call(
        functools.partial(backward_kernel, zs, bs, chunks, gathered),
        out_shape=(grad, grad, jax.ShapeDtypeStruct(tile, F32)),
        in_specs=[vmem] * 5,
        out_specs=(vmem,) * 3,
        scratch_shapes=[
            buf(chunks, zs, quads, 2, 2), buf(chunks, zs, quads, 2, 2),
            buf(chunks, zs, quads, 2), buf(chunks, zs, quads, 2),
            pltpu.VMEM(tile, F32), pltpu.VMEM((1,) + tile, F32),
            pltpu.VMEM((quads - 1,) + tile, F32), pltpu.VMEM((zs - 1,) + tile, F32),
            pltpu.SemaphoreType.DMA((chunks, 2, kinds)),
            pltpu.SemaphoreType.DMA((chunks, 2, kinds)),
            pltpu.SemaphoreType.DMA((kinds,)),
            pltpu.SemaphoreType.DMA((kinds,)),
        ] + [buf(*shape) for _, shape in layout(zs, bs, chunks)[1]],
        compiler_params=pltpu.CompilerParams(collective_id=0, has_side_effects=True),
    )(x, d, wi, wo, partial_loss)


def on_device(state, target, land_mask, batch_map, diffusion, speed_x, speed_y, w_in, w_out):
    feats, rows_x, rows_y = state.shape
    field = transported(state, diffusion, speed_x, speed_y)
    local_cols = rows_x * rows_y
    total = local_cols * lax.axis_size("bx") * lax.axis_size("by")
    flat = field.reshape(local_cols, feats)
    x = flat.astype(BF16)
    pre = jnp.dot(x, w_in, preferred_element_type=F32)
    hidden = jax.nn.silu(pre).astype(BF16)
    tend = jnp.dot(hidden, w_out, preferred_element_type=F32)
    weights = land_mask.reshape(local_cols).astype(F32)[:, None]
    err = weights * (tend - target.reshape(feats, local_cols).T.astype(F32))
    new_state = (flat + 0.5 * (weights * tend)).T.reshape(feats, rows_x, rows_y)
    persq = 0.5 * jnp.sum(err * err, axis=1)
    width = -(-BATCHES // 128) * 128
    onehot = (
        batch_map.reshape(local_cols)[:, None] == jnp.arange(width, dtype=jnp.int32)[None, :]
    ).astype(F32)
    partial_loss = jnp.dot(persq, onehot, precision=lax.Precision.HIGHEST) * (
        BATCHES / (total * feats)
    )
    d = (err * total ** (-0.5)).astype(BF16)
    grad_in, grad_out, loss = backward(
        x, d, w_in, w_out, jnp.broadcast_to(partial_loss[None, :], (8, width))
    )
    return (new_state, grad_in, grad_out, loss[0, :BATCHES])


def solution(mesh):
    placed = (
        P(None, "bx", "by"),
        P(None, "bx", "by"),
        P("bx", "by"),
        P("bx", "by"),
        P(),
        P(),
        P(),
        P(),
        P(),
    )
    return jax.shard_map(
        on_device,
        mesh=mesh,
        in_specs=placed,
        out_specs=(P(None, "bx", "by"), P(("bx", "by"), None), P(("bx", "by"), None), P()),
        check_vma=False,
    )
```

```python
import functools

import jax
import jax.numpy as jnp
from jax import lax
from jax.experimental import pallas as pl
from jax.experimental.pallas import tpu as pltpu
from jax.sharding import PartitionSpec as P

SUB = 3
BATCHES = 64
ACROSS_FIRST = ()
MESH = pl.DeviceIdType.MESH
F32 = jnp.float32
BF16 = jnp.bfloat16


WIDE = 8
EDGE = 2 * WIDE
SIDES = [(dx, dy) for dx in (-1, 0, 1) for dy in (-1, 0, 1) if dx or dy]


def halo_kernel(zs, bs, cells, kap_ref, sx_ref, sy_ref, out, out_x, first, second, send, recv):
    rows, depth, feats = cells.shape
    me_z, me_b = lax.axis_index("bx"), lax.axis_index("by")
    window = pl.ds(EDGE, depth)

    def has(side):
        dx, dy = side
        found = []
        if dx:
            found.append(me_z > 0 if dx < 0 else me_z < zs - 1)
        if dy:
            found.append(me_b > 0 if dy < 0 else me_b < bs - 1)
        return functools.reduce(jnp.logical_and, found)

    for buf in (first, second):
        for i in range(rows + 2 * SUB):
            buf[i, :EDGE] = jnp.zeros((EDGE, feats), F32)
            buf[i, EDGE + depth:] = jnp.zeros((EDGE, feats), F32)
    for i in list(range(SUB)) + list(range(rows + SUB, rows + 2 * SUB)):
        first[i, window] = jnp.zeros((depth, feats), F32)

    barrier = pltpu.get_barrier_semaphore()
    for dx, dy in SIDES:
        @pl.when(has((dx, dy)))
        def _():
            pl.semaphore_signal(
                barrier, inc=1, device_id=(me_z + dx, me_b + dy), device_id_type=MESH
            )
    near_z = jnp.where(me_z > 0, 1, 0) + jnp.where(me_z < zs - 1, 1, 0)
    near_b = jnp.where(me_b > 0, 1, 0) + jnp.where(me_b < bs - 1, 1, 0)
    pl.semaphore_wait(barrier, near_z + near_b + near_z * near_b)

    def own(side):
        dx, dy = side
        i = {-1: pl.ds(0, SUB), 0: pl.ds(0, rows), 1: pl.ds(rows - SUB, SUB)}[dx]
        j = {-1: pl.ds(0, WIDE), 0: pl.ds(0, depth), 1: pl.ds(depth - WIDE, WIDE)}[dy]
        return cells.at[i, j]

    def slot(side):
        dx, dy = side
        i = {-1: pl.ds(0, SUB), 0: pl.ds(SUB, rows), 1: pl.ds(SUB + rows, SUB)}[dx]
        j = {-1: pl.ds(WIDE, WIDE), 0: window, 1: pl.ds(EDGE + depth, WIDE)}[dy]
        return first.at[i, j]

    def copy_to(side):
        dx, dy = side
        back = (-dx, -dy)
        return pltpu.make_async_remote_copy(
            src_ref=own(side), dst_ref=slot(back),
            send_sem=send.at[SIDES.index(side)], recv_sem=recv.at[SIDES.index(back)],
            device_id=(me_z + dx, me_b + dy), device_id_type=MESH,
        )

    for side in sorted(SIDES, key=lambda s: (s[1] != 0, s[0] == 0)):
        @pl.when(has(side))
        def _():
            copy_to(side).start()
    for i in range(rows):
        first[SUB + i, window] = cells[i]
    for side in SIDES:
        @pl.when(has(side))
        def _():
            copy_to((-side[0], -side[1])).wait_recv()
    for side in SIDES:
        @pl.when(has(side))
        def _():
            copy_to(side).wait_send()

    kap, sxx, syy = kap_ref[...], sx_ref[...], sy_ref[...]
    low = jnp.where(me_b > 0, 1.0, 0.0).astype(F32)
    high = jnp.where(me_b < bs - 1, 1.0, 0.0).astype(F32)

    def moved(src, i, start, count):
        centre = src[i, pl.ds(start, count)]
        east = src[i + 1, pl.ds(start, count)]
        west = src[i - 1, pl.ds(start, count)]
        north = src[i, pl.ds(start + 1, count)]
        south = src[i, pl.ds(start - 1, count)]
        return (
            centre
            + kap * (east + west + north + south - 4.0 * centre)
            - 0.5 * sxx * (east - west)
            - 0.5 * syy * (north - south)
        )

    for step in range(SUB):
        src, dst = ((first, second), (second, first))[step % 2]
        margin = SUB - step - 1

        @pl.loop(SUB - margin, SUB + rows + margin)
        def _(i):
            if margin == 0:
                value = moved(src, i, EDGE, depth)
                out[i - SUB] = value
                out_x[i - SUB] = value.astype(BF16)
            else:
                at = me_z * rows + i - SUB
                inside = jnp.where((at >= 0) & (at < rows * zs), 1.0, 0.0).astype(F32)
                dst[i, pl.ds(WIDE, WIDE)] = moved(src, i, WIDE, WIDE) * (inside * low)
                dst[i, window] = moved(src, i, EDGE, depth) * inside
                dst[i, pl.ds(EDGE + depth, WIDE)] = moved(src, i, EDGE + depth, WIDE) * (
                    inside * high
                )


def transported(state, diffusion, speed_x, speed_y):
    zs, bs = lax.axis_size("bx"), lax.axis_size("by")
    cells = state.transpose(1, 2, 0)
    rows, depth, feats = cells.shape
    vmem = pl.BlockSpec(memory_space=pltpu.VMEM)
    padded = pltpu.VMEM((rows + 2 * SUB, depth + 2 * EDGE, feats), F32)
    return pl.pallas_call(
        functools.partial(halo_kernel, zs, bs),
        out_shape=(
            jax.ShapeDtypeStruct(cells.shape, F32), jax.ShapeDtypeStruct(cells.shape, BF16)
        ),
        in_specs=[vmem] * 4,
        out_specs=(vmem,) * 2,
        scratch_shapes=[
            padded, padded,
            pltpu.SemaphoreType.DMA((len(SIDES),)), pltpu.SemaphoreType.DMA((len(SIDES),)),
        ],
        compiler_params=pltpu.CompilerParams(collective_id=1, has_side_effects=True),
    )(cells, diffusion[None, :], speed_x[None, :], speed_y[None, :])


def tree(parts):
    if len(parts) == 1:
        return parts[0]
    return tree(parts[::2]) + tree(parts[1::2])


def chunk_count(block):
    return 8 if block % 64 == 0 else 4


def orders(chunks):
    plan = {}
    for c in range(chunks):
        for m in range(2):
            plane = "qa" if m == 0 else "aq"
            plan[m, c] = "z" + plane if c in ACROSS_FIRST else plane + "z"
    return plan


def layout(zs, bs, chunks):
    size = {"z": zs, "a": bs // 4, "q": 2}
    groups = {}
    for key, order in sorted(orders(chunks).items()):
        groups.setdefault(order, []).append(key)
    shapes = []
    for order, members in sorted(groups.items()):
        left = "zaq"
        for axis in order:
            left = left.replace(axis, "")
            shapes.append((order, (len(members), size[axis] - 1) + tuple(size[k] for k in left)))
    return groups, shapes


def backward_kernel(
    zs, bs, chunks, gathered,
    x_ref, d_ref, wi_ref, wo_ref, loss_ref,
    gin_ref, gout_ref, total_ref,
    g0, g1, c0, c1, lc, lq, la, lz,
    send, recv, lsend, lrecv, *stages,
):
    quads = bs // 4
    size = {"z": zs, "a": quads, "q": 2}
    me_z, me_b = lax.axis_index("bx"), lax.axis_index("by")
    core, q, a = lax.rem(me_b, 2), lax.rem(me_b // 2, 2), me_b // 4
    mine = {"z": me_z, "a": a, "q": q}
    rows, feats = g0.shape[-2:]
    grads, cores = (g0, g1), (c0, c1)
    outs = (gout_ref, gin_ref)
    plan = orders(chunks)
    groups, shapes = layout(zs, bs, chunks)
    landing = {}
    for (order, _), ref in zip(shapes, stages):
        landing.setdefault(order, []).append(ref)

    def other(axis, s):
        return lax.rem(mine[axis] + s, size[axis])

    core_peer = (me_z, me_b + 1 - 2 * core)
    peers = {
        "q": [(me_z, me_b + 2 - 4 * q)],
        "a": [(me_z, other("a", s) * 4 + lax.rem(me_b, 4)) for s in range(1, quads)],
        "z": [(other("z", s), me_b) for s in range(1, zs)],
    }
    everyone = [core_peer] + peers["q"] + peers["a"] + peers["z"]
    base = {"q": 1, "a": 2, "z": 2 + quads - 1}

    barrier = pltpu.get_barrier_semaphore()
    for peer in everyone:
        pl.semaphore_signal(barrier, inc=1, device_id=peer, device_id_type=MESH)

    def remote(src, dst, peer, ssem, rsem):
        return pltpu.make_async_remote_copy(
            src_ref=src, dst_ref=dst, send_sem=ssem, recv_sem=rsem,
            device_id=peer, device_id_type=MESH,
        )

    def held(stage, m, c):
        if stage == 1:
            return cores[m], (c,), "zaq"
        order = plan[m, c]
        left = "".join(k for k in "zaq" if k not in order[: stage - 1])
        return landing[order][stage - 2], (groups[order].index((m, c)), 0), left

    def part(lead, left, axis, at):
        return lead + tuple(at if k == axis else slice(None) for k in left)

    def copies(stage, m, c):
        if stage == 0:
            return [
                remote(
                    grads[m].at[c, :, :, :, 1 - core], cores[m].at[c], core_peer,
                    send.at[c, m, 0], recv.at[c, m, 0],
                )
            ]
        order = plan[m, c]
        axis = order[stage - 1]
        ref, lead, left = held(stage, m, c)
        spot = groups[order].index((m, c))
        return [
            remote(
                ref.at[part(lead, left, axis, other(axis, s))],
                landing[order][stage - 1].at[spot, s - 1],
                peers[axis][s - 1],
                send.at[c, m, base[axis] + s - 1], recv.at[c, m, base[axis] + s - 1],
            )
            for s in range(1, size[axis])
        ]

    def gather_sum(stage, m, c):
        if stage == 0:
            @pl.loop(0, zs)
            def _(z):
                cores[m][c, z] = cores[m][c, z] + grads[m][c, z, :, :, core]
            return
        order = plan[m, c]
        axis = order[stage - 1]
        ref, lead, left = held(stage, m, c)
        spot = groups[order].index((m, c))
        came = landing[order][stage - 1]
        summed = tree(
            [ref[part(lead, left, axis, mine[axis])]]
            + [came[spot, s] for s in range(size[axis] - 1)]
        )
        if stage == 3:
            outs[m][c * rows:(c + 1) * rows] = summed
        else:
            came[spot, 0] = summed

    loss_axes = "qaz"
    loss_from = [loss_ref, lc, lq.at[0], la.at[0]]
    loss_into = [lc, lq, la, lz]

    def loss_copies(stage):
        if stage == 0:
            return [remote(loss_ref, lc, core_peer, lsend.at[0], lrecv.at[0])]
        axis = loss_axes[stage - 1]
        return [
            remote(
                loss_from[stage], loss_into[stage].at[s - 1], peers[axis][s - 1],
                lsend.at[base[axis] + s - 1], lrecv.at[base[axis] + s - 1],
            )
            for s in range(1, size[axis])
        ]

    def loss_sum(stage):
        if stage == 0:
            lc[...] = lc[...] + loss_ref[...]
            return
        came = loss_into[stage]
        summed = tree(
            [loss_from[stage][...]]
            + [came[s] for s in range(size[loss_axes[stage - 1]] - 1)]
        )
        if stage == 3:
            total_ref[...] = summed
        else:
            came[0] = summed

    def transposed_dot(lhs, rhs):
        return lax.dot_general(lhs, rhs, (((1,), (1,)), ((), ())), preferred_element_type=F32)

    def compute(c):
        @pl.loop(0, zs)
        def _(z):
            if gathered:
                wi = wi_ref[pl.ds(z * bs, bs), c].reshape(bs * rows, feats)
                wo = wo_ref[pl.ds(z * bs, bs), c].reshape(bs * rows, feats)
            else:
                wi, wo = wi_ref[c * zs + z], wo_ref[c * zs + z]
            pre = transposed_dot(wi, x_ref[...])
            sig = jax.nn.sigmoid(pre)
            hidden = (pre * sig).astype(BF16)
            g0[c, z] = jnp.dot(hidden, d_ref[...], preferred_element_type=F32).reshape(
                quads, 2, 2, rows, feats
            )
            dhid = transposed_dot(wo, d_ref[...])
            dpre = (dhid * sig * (1.0 + pre * (1.0 - sig))).astype(BF16)
            g1[c, z] = jnp.dot(dpre, x_ref[...], preferred_element_type=F32).reshape(
                quads, 2, 2, rows, feats
            )

    started = []

    def begin(group):
        for copy in group:
            copy.start()
            started.append(copy)
        return group

    flying = {}
    for step in range(chunks + 4):
        if step < chunks:
            compute(step)
            if step == 0:
                pl.semaphore_wait(barrier, len(everyone))
            for m in range(2):
                flying[0, m, step] = begin(copies(0, m, step))
        if step == 0:
            flying["loss", 0] = begin(loss_copies(0))
        for stage in range(4):
            c = step - 1 - stage
            if not 0 <= c < chunks:
                continue
            for m in range(2):
                for copy in flying[stage, m, c]:
                    copy.wait_recv()
                gather_sum(stage, m, c)
                if stage < 3:
                    flying[stage + 1, m, c] = begin(copies(stage + 1, m, c))
            if c == 0:
                for copy in flying["loss", stage]:
                    copy.wait_recv()
                loss_sum(stage)
                if stage < 3:
                    flying["loss", stage + 1] = begin(loss_copies(stage + 1))
    for copy in started:
        copy.wait_send()


def backward(x, d, wi, wo, partial_loss):
    zs, bs = lax.axis_size("bx"), lax.axis_size("by")
    quads = bs // 4
    hid, feats = wo.shape
    blocks = zs * bs
    chunks = chunk_count(hid // blocks)
    rows = hid // blocks // chunks
    gathered = rows % 16 == 0
    wi = wi.T.reshape(blocks, chunks, rows, feats)
    wo = wo.reshape(blocks, chunks, rows, feats)
    if not gathered:
        wi, wo = (
            w.transpose(1, 0, 2, 3).reshape(chunks * zs, bs * rows, feats) for w in (wi, wo)
        )
    kinds = 2 + (quads - 1) + (zs - 1)
    vmem = pl.BlockSpec(memory_space=pltpu.VMEM)
    tile = partial_loss.shape

    def buf(*shape):
        return pltpu.VMEM(shape + (rows, feats), F32)

    grad = jax.ShapeDtypeStruct((rows * chunks, feats), F32)
    return pl.pallas_call(
        functools.partial(backward_kernel, zs, bs, chunks, gathered),
        out_shape=(grad, grad, jax.ShapeDtypeStruct(tile, F32)),
        in_specs=[vmem] * 5,
        out_specs=(vmem,) * 3,
        scratch_shapes=[
            buf(chunks, zs, quads, 2, 2), buf(chunks, zs, quads, 2, 2),
            buf(chunks, zs, quads, 2), buf(chunks, zs, quads, 2),
            pltpu.VMEM(tile, F32), pltpu.VMEM((1,) + tile, F32),
            pltpu.VMEM((quads - 1,) + tile, F32), pltpu.VMEM((zs - 1,) + tile, F32),
            pltpu.SemaphoreType.DMA((chunks, 2, kinds)),
            pltpu.SemaphoreType.DMA((chunks, 2, kinds)),
            pltpu.SemaphoreType.DMA((kinds,)),
            pltpu.SemaphoreType.DMA((kinds,)),
        ] + [buf(*shape) for _, shape in layout(zs, bs, chunks)[1]],
        compiler_params=pltpu.CompilerParams(collective_id=0, has_side_effects=True),
    )(x, d, wi, wo, partial_loss)


def on_device(state, target, land_mask, batch_map, diffusion, speed_x, speed_y, w_in, w_out):
    feats, rows_x, rows_y = state.shape
    field, field_x = transported(state, diffusion, speed_x, speed_y)
    local_cols = rows_x * rows_y
    total = local_cols * lax.axis_size("bx") * lax.axis_size("by")
    flat = field.reshape(local_cols, feats)
    x = field_x.reshape(local_cols, feats)
    pre = jnp.dot(x, w_in, preferred_element_type=F32)
    hidden = jax.nn.silu(pre).astype(BF16)
    tend = jnp.dot(hidden, w_out, preferred_element_type=F32)
    weights = land_mask.reshape(local_cols).astype(F32)[:, None]
    err = weights * (tend - target.reshape(feats, local_cols).T.astype(F32))
    new_state = (flat + 0.5 * (weights * tend)).T.reshape(feats, rows_x, rows_y)
    persq = 0.5 * jnp.sum(err * err, axis=1)
    width = -(-BATCHES // 128) * 128
    onehot = (
        batch_map.reshape(local_cols)[:, None] == jnp.arange(width, dtype=jnp.int32)[None, :]
    ).astype(F32)
    partial_loss = jnp.dot(persq, onehot, precision=lax.Precision.HIGHEST) * (
        BATCHES / (total * feats)
    )
    d = (err * total ** (-0.5)).astype(BF16)
    grad_in, grad_out, loss = backward(
        x, d, w_in, w_out, jnp.broadcast_to(partial_loss[None, :], (8, width))
    )
    return (new_state, grad_in, grad_out, loss[0, :BATCHES])


def solution(mesh):
    placed = (
        P(None, "bx", "by"),
        P(None, "bx", "by"),
        P("bx", "by"),
        P("bx", "by"),
        P(),
        P(),
        P(),
        P(),
        P(),
    )
    return jax.shard_map(
        on_device,
        mesh=mesh,
        in_specs=placed,
        out_specs=(P(None, "bx", "by"), P(("bx", "by"), None), P(("bx", "by"), None), P()),
        check_vma=False,
    )
```
